256 devices in a mesh: slab: 64 (over z, y, core), quad: 4 (over x).
Axes of the slice: x: 4, y: 4, z: 8, core: 2. Of those that a mesh axis runs over, the one named last changes fastest.
Arguments:
- grain_cell: int32 [4, 2097152], P(None, ('slab', 'quad')), may hold values from 0 to 254, as said below
- grain_count: int32 [256], P(('slab', 'quad')), may hold values from 2048 to 8192, as said below
- grain_weight: float32 [2097152], P(('slab', 'quad')), may hold values from 0.05 to 0.95
- grain_volume: float32 [2097152], P(('slab', 'quad')), may hold values from 0.02 to 0.4
- grain_velocity: float32 [3, 2097152], P(None, ('slab', 'quad')), may hold values from -6 to 6
Outputs:
- pressure: float32 [256, 64, 256], P('slab', 'quad')
- drag: float32 [3, 2097152], P(None, ('slab', 'quad'))
The draws below stay inside these ranges and needn't reach their ends.
Inputs may be any that keep to these rules, and one draw needn't show every extreme that they name: grain_cell[0] < 4, grain_cell[1] < 4, grain_cell[2] < 16, grain_cell[3] <= 254; among the slots of one device at most 4096 name the same quarter, and on every device exactly 4096 name one quarter. `grain_count`: some device has all 8192 slots occupied.
All inputs are finite; a program needn't handle non-finite values.
Results may differ from the reference program's by a relative error of at most 0.00002.
Values sent between devices are 32-bit elements; how exact they have to be, the bound alone decides.
A program may use at most 128 MiB of HBM per device.

```python
import math
import jax
import jax.numpy as jnp
from jax import lax

CH = 4
CA = 16
CB = 256
GR_DEV = 8192
ITERS = 12
GRAINS = 2097152
N_SLAB = 64
N_QUAD = 4


def quarter_block(key):
    keys = jax.random.split(key, 3)
    heavy = jax.random.randint(keys[0], (), 0, N_QUAD)
    others = jax.random.randint(keys[1], (GR_DEV,), 1, N_QUAD)
    spread = (heavy + others) % N_QUAD
    index = jnp.arange(GR_DEV, dtype=jnp.int32)
    chosen = jnp.where(index < GR_DEV // 2, heavy, spread)
    return jax.random.permutation(keys[2], chosen)


def draw_grain_cell(key, part):
    keys = jax.random.split(key, 4)
    device_keys = jax.random.split(keys[0], N_SLAB * N_QUAD)
    quarter = jax.vmap(quarter_block)(device_keys).reshape(GRAINS)
    layer = jax.random.randint(keys[1], (GRAINS,), 0, CH)
    across = jax.random.randint(keys[2], (GRAINS,), 0, CA)
    along = jax.random.randint(keys[3], (GRAINS,), 0, CB - 1)
    return jnp.stack([quarter, layer, across, along]).astype(jnp.int32)


def draw_grain_count(key, part):
    keys = jax.random.split(key, 2)
    counts = jax.random.randint(keys[0], (N_SLAB * N_QUAD,), GR_DEV // 4, GR_DEV + 1)
    fullest = jax.random.randint(keys[1], (), 0, N_SLAB * N_QUAD)
    return counts.at[fullest].set(GR_DEV).astype(jnp.int32)


def level_of(stream_key, dims, cuts, least, high):
    level, own = 1.0, jax.random.fold_in(stream_key, 6)
    for dim, parts in cuts:
        draws = jnp.exp(jax.random.uniform(jax.random.fold_in(own, dim), (parts,), jnp.float32, least / len(cuts), high / len(cuts)))
        level = level * jnp.repeat(draws, dims[dim] // parts).reshape([-1 if axis == dim else 1 for axis in range(len(dims))])
    return level


def noise(own_key, dims, width, most, pieces=(), kind=jnp.bfloat16):
    factor_of = level_of(own_key, dims, pieces, -0.22, 0.18) if pieces else 1.0
    result = jax.random.normal(own_key, dims, jnp.float32) * width * factor_of
    return jnp.minimum(jnp.maximum(result, -most), most).astype(kind)


def setup_inputs(seed: int = 0) -> dict:
    streams_of = jax.random.split(jax.random.key(seed), 6)
    grain_cell = draw_grain_cell(jax.random.fold_in(streams_of[5], 71), 0)
    grain_count = draw_grain_count(jax.random.fold_in(streams_of[5], 71), 0)
    grain_weight = jnp.clip(0.05 + 0.9 * jax.random.uniform(streams_of[2], (GRAINS,), jnp.float32) ** level_of(streams_of[2], (GRAINS,), ((0, 256),), -0.2, 0.2), 0.05, 0.95)
    grain_volume = jnp.clip(jnp.exp(math.log(0.4) - 2.9957323 * jax.random.uniform(streams_of[3], (GRAINS,), jnp.float32) ** level_of(streams_of[3], (GRAINS,), ((0, 256),), -0.2, 0.2)), 0.02, 0.4)
    grain_velocity = noise(streams_of[4], (3, GRAINS), 1.0, 6.0, ((1, 256),), jnp.float32)
    return {"grain_cell": grain_cell, "grain_count": grain_count, "grain_weight": grain_weight, "grain_volume": grain_volume, "grain_velocity": grain_velocity}


damping = 0.05
source_gain = 4.0


def neighbours(padded):
    centre = padded[1:-1, 1:-1]
    along = jnp.pad(centre, ((0, 0), (0, 0), (1, 1)))
    total = padded[2:, 1:-1] + padded[:-2, 1:-1] + padded[1:-1, 2:] + padded[1:-1, :-2]
    return total + along[:, :, 2:] + along[:, :, :-2]


def gradient(wide):
    vel_height = -0.5 * (wide[2:, 1:-1, 1:-1] - wide[:-2, 1:-1, 1:-1])
    vel_across = -0.5 * (wide[1:-1, 2:, 1:-1] - wide[1:-1, :-2, 1:-1])
    vel_along = -0.5 * (wide[1:-1, 1:-1, 2:] - wide[1:-1, 1:-1, :-2])
    return vel_height, vel_across, vel_along


def reference(grain_cell, grain_count, grain_weight, grain_volume, grain_velocity):
    heights = CH * N_SLAB
    across = CA * N_QUAD
    cells = heights * across * CB
    slots = jnp.arange(GRAINS, dtype=jnp.int32)
    owner = (slots // GR_DEV).astype(jnp.int32)
    valid = ((slots % GR_DEV) < grain_count[owner]).astype(jnp.float32)
    slab_of = owner // N_QUAD
    height = slab_of * CH + grain_cell[1]
    flat = ((height * across + grain_cell[0] * CA + grain_cell[2]) * CB + grain_cell[3]).astype(jnp.int32)
    mass = valid * grain_volume
    lower = grain_weight
    upper = 1.0 - grain_weight
    amounts = jnp.stack([mass, mass * grain_velocity[0]])
    field = jnp.zeros((2, cells), jnp.float32)
    field = field.at[:, flat].add(amounts * lower).at[:, flat + 1].add(amounts * upper)
    field = field.reshape(2, heights, across, CB)
    solid = field[0]
    voidage = 1.0 / (1.0 + solid)
    source = source_gain * field[1]

    def relax(repeat, pressure):
        padded = jnp.pad(pressure, ((1, 1), (1, 1), (0, 0)))
        return (source + voidage * neighbours(padded)) / (6.0 * voidage + damping)

    pressure = lax.fori_loop(0, ITERS, relax, jnp.zeros((heights, across, CB), jnp.float32))
    vel_height, vel_across, vel_along = gradient(jnp.pad(pressure, 1))
    table = jnp.stack([vel_height, vel_across, vel_along, solid]).reshape(4, cells)
    sampled = lower * table[:, flat] + upper * table[:, flat + 1]
    factor = mass * (1.0 + sampled[3]) ** 2
    drag = factor * (sampled[:3] - grain_velocity)
    return pressure, drag
```

```python
import functools

import jax
import jax.numpy as jnp
from jax import lax
from jax.experimental import pallas as pl
from jax.experimental.pallas import tpu as pltpu
from jax.sharding import PartitionSpec as P

CH = 4
CA = 16
CB = 256
QUADS = 4
ROWS = CH * CA * QUADS
ACROSS = CA * QUADS
PAD = 8
CHUNK = CB // QUADS
GBLOCK = 1024
GTILE = 256

F32 = jnp.float32
BF16 = jnp.bfloat16


def split(x):
    high = x.astype(BF16)
    return high, (x - high.astype(F32)).astype(BF16)


def row_index(cell):
    return cell[1:2] * ACROSS + cell[0:1] * CA + cell[2:3]


def one_hot_rows(rows, width):
    wanted = lax.broadcasted_iota(jnp.int32, (ROWS, width), 0)
    return jnp.where(wanted == rows, 1.0, 0.0).astype(BF16)


def masses(count_ref, vol, start, width):
    slots = start + lax.broadcasted_iota(jnp.int32, (1, width), 1)
    return jnp.where(slots < count_ref[0], vol, 0.0)


def deposit_kernel(count_ref, cell_ref, weight_ref, volume_ref, velocity_ref, out_ref):
    step = pl.program_id(0)

    @pl.when(step == 0)
    def _():
        out_ref[...] = jnp.zeros_like(out_ref)

    cell = cell_ref[...]
    weight = weight_ref[...]
    mass = masses(count_ref, volume_ref[...], step * GBLOCK, GBLOCK)
    upper = 1.0 - weight
    along = cell[3:4]
    rows = one_hot_rows(row_index(cell), GBLOCK)
    wanted = lax.broadcasted_iota(jnp.int32, (CB, GBLOCK), 0)
    lower_hit = wanted == along
    upper_hit = wanted == along + 1
    for field, amount in enumerate((mass, mass * velocity_ref[0:1])):
        low_hi, low_lo = split(amount * weight)
        up_hi, up_lo = split(amount * upper)
        total = None
        for low, up in ((low_hi, up_hi), (low_lo, up_lo)):
            spread = jnp.where(
                lower_hit, low.astype(F32), jnp.where(upper_hit, up.astype(F32), 0.0)
            ).astype(BF16)
            part = lax.dot_general(
                spread, rows, (((1,), (1,)), ((), ())), preferred_element_type=F32
            )
            total = part if total is None else total + part
        for pair in range(2):
            out_ref[field, pair] += total[:, pair * 128 : (pair + 1) * 128]


def relax_kernel(
    slabs,
    d_ref,
    p_ref,
    s_ref,
    gathered,
    coef,
    a_ref,
    b_ref,
    x0,
    x1,
    y0,
    z0,
    rs_send,
    rs_recv,
    ag_send,
    ag_recv,
    halo_send,
    halo_recv,
    p_send,
    p_recv,
):
    quad = lax.axis_index("quad")
    slab = lax.axis_index("slab")
    nexts = lax.rem(slab + 1, slabs)
    prevs = lax.rem(slab + slabs - 1, slabs)
    peers = [lax.rem(quad + d, QUADS) for d in range(QUADS)]
    origins = [lax.rem(quad + QUADS - d, QUADS) for d in range(QUADS)]

    def at(q, s):
        return {"quad": q, "slab": s}

    def rows_of(q):
        return pl.ds(pl.multiple_of(q * CHUNK, CHUNK), CHUNK)

    barrier = pltpu.get_barrier_semaphore()
    partners = [at(peers[d], slab) for d in range(1, QUADS)]
    partners += [at(quad, nexts), at(quad, prevs)]
    for partner in partners:
        pl.semaphore_signal(
            barrier, inc=1, device_id=partner, device_id_type=pl.DeviceIdType.MESH
        )
    for buffer in (x0, x1, y0, z0, p_ref):
        zero = jnp.zeros((buffer.shape[0], PAD, 128), F32)
        buffer[:, 0:PAD, :] = zero
        buffer[:, PAD + CB :, :] = zero
    pl.semaphore_wait(barrier, len(partners))

    def send(src, dst, ssem, rsem, where):
        copy = pltpu.make_async_remote_copy(
            src_ref=src,
            dst_ref=dst,
            send_sem=ssem,
            recv_sem=rsem,
            device_id=where,
            device_id_type=pl.DeviceIdType.MESH,
        )
        copy.start()
        return copy

    scatter = []
    for d in (2, 1, 3):
        scatter.append(
            send(
                d_ref.at[:, :, rows_of(peers[d]), :],
                gathered.at[d - 1],
                rs_send.at[d - 1],
                rs_recv.at[d - 1],
                at(peers[d], slab),
            )
        )
    own = rows_of(quad)
    for copy in scatter:
        copy.wait_recv()
    coef[:, 2:4, own, :] = (d_ref[:, :, own, :] + gathered[0]) + (gathered[1] + gathered[2])

    mine = coef.at[:, 2:4, own, :]
    gather = {}
    for d in (2, 1, 3):
        gather[d] = send(mine, mine, ag_send.at[d - 1], ag_recv.at[d - 1], at(peers[d], slab))
    halos = []

    def forward(d):
        block = rows_of(origins[d])
        src = coef.at[:, 2:4, block, :]
        halos.append(
            send(src, coef.at[:, 0:2, block, :], halo_send.at[0, d], halo_recv.at[0, d], at(quad, nexts))
        )
        halos.append(
            send(src, coef.at[:, 4:6, block, :], halo_send.at[1, d], halo_recv.at[1, d], at(quad, prevs))
        )

    forward(0)
    for d in (1, 3, 2):
        gather[d].wait_recv()
        forward(d)
    for copy in halos:
        copy.wait_recv()

    not_first = jnp.where(slab > 0, 1.0, 0.0)
    not_last = jnp.where(slab < slabs - 1, 1.0, 0.0)

    def coefficients(k, carry):
        live = jnp.where(k < 2, not_first, jnp.where(k > 3, not_last, 1.0))
        for r in range(0, CB, 64):
            thick = 1.0 + coef[0, k, r : r + 64, :]
            ratio = live / (6.0 + 0.05 * thick)
            source = 4.0 * coef[1, k, r : r + 64, :] * thick * ratio
            b_ref[k, r : r + 64, :] = ratio
            a_ref[k, r : r + 64, :] = source
            x0[k, PAD + r : PAD + r + 64, :] = source
        return carry

    lax.fori_loop(0, 6, coefficients, 0)
    for k in range(2):
        s_ref[k] = coef[0, 2 + k]

    lane = lax.broadcasted_iota(jnp.int32, (64, 128), 1)
    second = lane >= 64
    place = lax.rem(lane, 64)
    has_low = place > 0
    has_high = place < 63

    def sweep(src, dst, start, stop, shift=0):
        def body(k, carry):
            below = jnp.maximum(k - 1, 0)
            above = jnp.minimum(k + 1, 5)
            for r in range(0, CB, 64):
                o = PAD + r
                here = src[k, o : o + 64, :]
                layers = here + jnp.where(second, src[below, o : o + 64, :], src[above, o : o + 64, :])
                total = pltpu.roll(layers, 64, axis=1)
                total += src[k, o - 1 : o + 63, :] + src[k, o + 1 : o + 65, :]
                total += jnp.where(has_low, pltpu.roll(here, 1, axis=1), 0.0)
                total += jnp.where(has_high, pltpu.roll(here, 127, axis=1), 0.0)
                dst[k - shift, o : o + 64, :] = (
                    a_ref[k, r : r + 64, :] + b_ref[k, r : r + 64, :] * total
                )
            return carry

        lax.fori_loop(start, stop, body, 0)

    def exchange(buffer, n):
        src = buffer.at[2:4, PAD : PAD + CB, :]
        copies = [
            send(src, buffer.at[0:2, PAD : PAD + CB, :], p_send.at[n, 0], p_recv.at[n, 0], at(quad, nexts)),
            send(src, buffer.at[4:6, PAD : PAD + CB, :], p_send.at[n, 1], p_recv.at[n, 1], at(quad, prevs)),
        ]
        for copy in copies:
            copy.wait_recv()

        @pl.when(slab == 0)
        def _():
            buffer[0:2, PAD : PAD + CB, :] = jnp.zeros((2, CB, 128), F32)

        @pl.when(slab == slabs - 1)
        def _():
            buffer[4:6, PAD : PAD + CB, :] = jnp.zeros((2, CB, 128), F32)

        return copies

    sweep(x0, x1, 0, 6)
    sweep(x1, x0, 1, 5)
    sweep(x0, x1, 1, 5)
    sweep(x1, y0, 2, 4)
    first = exchange(y0, 0)
    sweep(y0, x0, 0, 6)
    sweep(x0, x1, 1, 5)
    sweep(x1, x0, 1, 5)
    sweep(x0, z0, 2, 4)
    later = exchange(z0, 1)
    sweep(z0, x0, 0, 6)
    sweep(x0, x1, 1, 5)
    sweep(x1, p_ref, 1, 5, shift=1)

    for copy in scatter + list(gather.values()) + halos + first + later:
        copy.wait_send()


def sample_kernel(
    count_ref,
    cell_ref,
    weight_ref,
    volume_ref,
    velocity_ref,
    p_ref,
    s_ref,
    pressure_ref,
    drag_ref,
    high_ref,
    low_ref,
    turned,
):
    step = pl.program_id(0)

    @pl.when(step == 0)
    def _():
        lane = lax.broadcasted_iota(jnp.int32, (CB, 128), 1)
        first = lane < 64
        place = lax.rem(lane, 64)
        for k in range(2):
            rows = slice(PAD, PAD + CB)
            here = p_ref[k + 1, rows, :]
            swap = [pltpu.roll(p_ref[k + j, rows, :], 64, axis=1) for j in range(3)]
            high = jnp.where(first, swap[1], swap[2])
            low = jnp.where(first, swap[0], swap[1])
            fields = [-0.5 * (high - low)]
            right = jnp.where(place < 63, pltpu.roll(here, 127, axis=1), 0.0)
            left = jnp.where(place > 0, pltpu.roll(here, 1, axis=1), 0.0)
            fields.append(-0.5 * (right - left))
            fields.append(
                -0.5 * (p_ref[k + 1, PAD + 1 : PAD + CB + 1, :] - p_ref[k + 1, PAD - 1 : PAD + CB - 1, :])
            )
            fields.append(s_ref[k])
            for f, field in enumerate(fields):
                hi, lo = split(field)
                high_ref[f * CB : (f + 1) * CB, k * 128 : (k + 1) * 128] = hi
                low_ref[f * CB : (f + 1) * CB, k * 128 : (k + 1) * 128] = lo
            turned[k * 128 : (k + 1) * 128, :] = here.T
        quad = lax.axis_index("quad")
        for layer in range(CH):
            at = pl.multiple_of(layer * ACROSS + quad * CA, CA)
            pressure_ref[layer] = turned[pl.ds(at, CA), :]

    def body(t, carry):
        base = pl.multiple_of(t * GTILE, GTILE)
        tile = pl.ds(base, GTILE)
        cell = cell_ref[:, tile]
        weight = weight_ref[:, tile]
        upper = 1.0 - weight
        mass = masses(count_ref, volume_ref[:, tile], step * GBLOCK + base, GTILE)
        rows = one_hot_rows(row_index(cell), GTILE)
        along = cell[3:4]
        wanted = lax.broadcasted_iota(jnp.int32, (CB, GTILE), 0)
        pick = jnp.where(wanted == along, weight, jnp.where(wanted == along + 1, upper, 0.0))
        sampled = []
        for f in range(4):
            block = slice(f * CB, (f + 1) * CB)
            picked = jnp.dot(high_ref[block, :], rows, preferred_element_type=F32)
            picked += jnp.dot(low_ref[block, :], rows, preferred_element_type=F32)
            sampled.append(jnp.sum(pick * picked, axis=0, keepdims=True))
        factor = mass * (1.0 + sampled[3]) ** 2
        for f in range(3):
            drag_ref[f : f + 1, tile] = factor * (sampled[f] - velocity_ref[f : f + 1, tile])
        return carry

    lax.fori_loop(0, GBLOCK // GTILE, body, 0)


def body(slabs, grain_cell, grain_count, grain_weight, grain_volume, grain_velocity):
    grains = grain_weight.shape[0]
    weight = grain_weight.reshape(1, grains)
    volume = grain_volume.reshape(1, grains)
    smem = pl.BlockSpec(memory_space=pltpu.SMEM)
    vmem = pl.BlockSpec(memory_space=pltpu.VMEM)
    grain_specs = [
        smem,
        pl.BlockSpec((4, GBLOCK), lambda i: (0, i)),
        pl.BlockSpec((1, GBLOCK), lambda i: (0, i)),
        pl.BlockSpec((1, GBLOCK), lambda i: (0, i)),
        pl.BlockSpec((3, GBLOCK), lambda i: (0, i)),
    ]
    steps = grains // GBLOCK
    deposits = pl.pallas_call(
        deposit_kernel,
        grid=(steps,),
        out_shape=jax.ShapeDtypeStruct((2, 2, CB, 128), F32),
        in_specs=grain_specs,
        out_specs=pl.BlockSpec((2, 2, CB, 128), lambda i: (0, 0, 0, 0)),
        name="deposit",
    )(grain_count, grain_cell, weight, volume, grain_velocity)
    dma = pltpu.SemaphoreType.DMA
    pressure, solid = pl.pallas_call(
        functools.partial(relax_kernel, slabs),
        out_shape=(
            jax.ShapeDtypeStruct((4, CB + 2 * PAD, 128), F32),
            jax.ShapeDtypeStruct((2, CB, 128), F32),
        ),
        in_specs=[vmem],
        out_specs=(vmem, vmem),
        scratch_shapes=[
            pltpu.VMEM((3, 2, 2, CHUNK, 128), F32),
            pltpu.VMEM((2, 6, CB, 128), F32),
            pltpu.VMEM((6, CB, 128), F32),
            pltpu.VMEM((6, CB, 128), F32),
        ]
        + [pltpu.VMEM((6, CB + 2 * PAD, 128), F32)] * 4
        + [dma((3,))] * 4
        + [dma((2, QUADS))] * 2
        + [dma((2, 2))] * 2,
        compiler_params=pltpu.CompilerParams(collective_id=0, has_side_effects=True),
        name="relax",
    )(deposits)
    return pl.pallas_call(
        sample_kernel,
        grid=(steps,),
        out_shape=(
            jax.ShapeDtypeStruct((CH, CA, CB), F32),
            jax.ShapeDtypeStruct((3, grains), F32),
        ),
        in_specs=grain_specs + [vmem, vmem],
        out_specs=(
            pl.BlockSpec((CH, CA, CB), lambda i: (0, 0, 0)),
            pl.BlockSpec((3, GBLOCK), lambda i: (0, i)),
        ),
        scratch_shapes=[
            pltpu.VMEM((4 * CB, ROWS), BF16),
            pltpu.VMEM((4 * CB, ROWS), BF16),
            pltpu.VMEM((ROWS, CB), F32),
        ],
        name="sample",
    )(grain_count, grain_cell, weight, volume, grain_velocity, pressure, solid)


def solution(mesh):
    placed = (
        P(None, ("slab", "quad")),
        P(("slab", "quad")),
        P(("slab", "quad")),
        P(("slab", "quad")),
        P(None, ("slab", "quad")),
    )
    return jax.shard_map(
        functools.partial(body, mesh.shape["slab"]),
        mesh=mesh,
        in_specs=placed,
        out_specs=(P("slab", "quad", None), P(None, ("slab", "quad"))),
        check_vma=False,
    )
```

```python
import functools

import jax
import jax.numpy as jnp
from jax import lax
from jax.experimental import pallas as pl
from jax.experimental.pallas import tpu as pltpu
from jax.sharding import PartitionSpec as P

CH = 4
CA = 16
CB = 256
QUADS = 4
ROWS = CH * CA * QUADS
ACROSS = CA * QUADS
PAD = 8
HALF = CB // 2
HELD = HALF + 2 * PAD
CHUNK = HALF // QUADS
GBLOCK = 1024
GTILE = 512
UNROLL = 4

F32 = jnp.float32
BF16 = jnp.bfloat16


def split(x):
    high = x.astype(BF16)
    return high, (x - high.astype(F32)).astype(BF16)


def row_index(cell):
    return cell[1:2] * ACROSS + cell[0:1] * CA + cell[2:3]


def small(x):
    return x.astype(F32).astype(BF16)


def one_hot_rows(rows, width):
    wanted = small(lax.broadcasted_iota(jnp.int32, (ROWS, width), 0))
    return jnp.where(wanted == small(rows), BF16(1.0), BF16(0.0))


def masses(count_ref, vol, start, width):
    slots = start + lax.broadcasted_iota(jnp.int32, (1, width), 1)
    return jnp.where(slots < count_ref[0], vol, 0.0)


def fold(top, bottom, first):
    return (
        jnp.where(first, top, pltpu.roll(bottom, 64, axis=1)),
        jnp.where(first, pltpu.roll(top, 64, axis=1), bottom),
    )


def deposit(count_ref, cell_ref, weight_ref, volume_ref, velocity_ref, out_ref, total, va, vb):
    total[...] = jnp.zeros_like(total)
    blocks = cell_ref.shape[1] // GBLOCK

    def tile_of(t):
        return pl.ds(pl.multiple_of(t * GBLOCK, GBLOCK), GBLOCK)

    def build(t, spread):
        tile = tile_of(t)
        weight = weight_ref[:, tile]
        mass = masses(count_ref, volume_ref[:, tile], t * GBLOCK, GBLOCK)
        upper = 1.0 - weight
        along = small(cell_ref[3:4, tile])
        above = along + BF16(1.0)
        shares = []
        for amount in (mass, mass * velocity_ref[0:1, tile]):
            shares += zip(split(amount * weight), split(amount * upper))
        for r in range(0, CB, 16):
            wanted = small(lax.broadcasted_iota(jnp.int32, (16, GBLOCK), 0) + r)
            lower_hit = wanted == along
            upper_hit = wanted == above
            for n, (low, up) in enumerate(shares):
                spread[n * CB + r : n * CB + r + 16, :] = jnp.where(
                    lower_hit, low, jnp.where(upper_hit, up, BF16(0.0))
                )

    def add(t, spread):
        rows = one_hot_rows(row_index(cell_ref[:, tile_of(t)]), GBLOCK)
        total[...] += lax.dot_general(
            spread[...], rows, (((1,), (1,)), ((), ())), preferred_element_type=F32
        )

    build(0, va)

    def body(i, carry):
        t = 2 * i
        build(t + 1, vb)
        add(t, va)
        build(jnp.minimum(t + 2, blocks - 1), va)
        add(t + 1, vb)
        return carry

    lax.fori_loop(0, blocks // 2, body, 0)
    first = lax.broadcasted_iota(jnp.int32, (HALF, 128), 1) < 64
    for field in range(2):
        for pair in range(2):
            lanes = slice(pair * 128, (pair + 1) * 128)
            r = field * 2 * CB
            whole = total[r : r + CB, lanes] + total[r + CB : r + 2 * CB, lanes]
            even, odd = fold(whole[:HALF], whole[HALF:], first)
            out_ref[field, 2 * pair] = even
            out_ref[field, 2 * pair + 1] = odd


def relax_kernel(
    slabs,
    count_ref,
    cell_ref,
    weight_ref,
    volume_ref,
    velocity_ref,
    p_ref,
    solid_ref,
    d_ref,
    total_ref,
    va,
    vb,
    high_ref,
    low_ref,
    gathered,
    coef,
    a_ref,
    b_ref,
    x0,
    x1,
    y0,
    z0,
    rs_send,
    rs_recv,
    ag_send,
    ag_recv,
    halo_send,
    halo_recv,
    p_send,
    p_recv,
):
    quad = lax.axis_index("quad")
    slab = lax.axis_index("slab")
    nexts = lax.rem(slab + 1, slabs)
    prevs = lax.rem(slab + slabs - 1, slabs)
    peers = [lax.rem(quad + d, QUADS) for d in range(QUADS)]
    origins = [lax.rem(quad + QUADS - d, QUADS) for d in range(QUADS)]

    def at(q, s):
        return {"quad": q, "slab": s}

    def rows_of(q):
        return pl.ds(pl.multiple_of(q * CHUNK, CHUNK), CHUNK)

    barrier = pltpu.get_barrier_semaphore()
    partners = [at(peers[d], slab) for d in range(1, QUADS)]
    partners += [at(quad, nexts), at(quad, prevs)]
    for partner in partners:
        pl.semaphore_signal(
            barrier, inc=1, device_id=partner, device_id_type=pl.DeviceIdType.MESH
        )
    deposit(count_ref, cell_ref, weight_ref, volume_ref, velocity_ref, d_ref, total_ref, va, vb)
    pl.semaphore_wait(barrier, len(partners))

    def send(src, dst, ssem, rsem, where):
        copy = pltpu.make_async_remote_copy(
            src_ref=src,
            dst_ref=dst,
            send_sem=ssem,
            recv_sem=rsem,
            device_id=where,
            device_id_type=pl.DeviceIdType.MESH,
        )
        copy.start()
        return copy

    scatter, gather, halos = [], [], []
    for f in range(2):
        scatter.append(
            {
                d: send(
                    d_ref.at[f, :, rows_of(peers[d]), :],
                    gathered.at[f, d - 1],
                    rs_send.at[f, d - 1],
                    rs_recv.at[f, d - 1],
                    at(peers[d], slab),
                )
                for d in (2, 1, 3)
            }
        )
    own = rows_of(quad)

    def forward(f, d):
        block = rows_of(origins[d])
        src = coef.at[f, 4:8, block, :]
        for side, (low, where) in enumerate(((0, nexts), (8, prevs))):
            halos.append(
                send(
                    src,
                    coef.at[f, low : low + 4, block, :],
                    halo_send.at[f, side, d],
                    halo_recv.at[f, side, d],
                    at(quad, where),
                )
            )

    for f in range(2):
        for copy in scatter[f].values():
            copy.wait_recv()
        coef[f, 4:8, own, :] = (d_ref[f, :, own, :] + gathered[f, 0]) + (
            gathered[f, 1] + gathered[f, 2]
        )
        mine = coef.at[f, 4:8, own, :]
        gather.append(
            {
                d: send(mine, mine, ag_send.at[f, d - 1], ag_recv.at[f, d - 1], at(peers[d], slab))
                for d in (2, 1, 3)
            }
        )
        forward(f, 0)
    for f in range(2):
        for d in (1, 3, 2):
            gather[f][d].wait_recv()
            forward(f, d)

    first = lax.broadcasted_iota(jnp.int32, (HALF, 128), 1) < 64
    for pair in range(2):
        store_split(fold(coef[0, 4 + 2 * pair], coef[0, 5 + 2 * pair], first), high_ref, low_ref, 0, pair)

    def keep(tile, sampled):
        solid_ref[:, tile] = sampled[0]

    sample(cell_ref, weight_ref, high_ref, low_ref, 1, keep)
    for copy in halos:
        copy.wait_recv()

    not_first = jnp.where(slab > 0, 1.0, 0.0)
    not_last = jnp.where(slab < slabs - 1, 1.0, 0.0)

    lane = lax.broadcasted_iota(jnp.int32, (HALF, 128), 1)
    place = lax.rem(lane, 64)
    has_low = place > 0
    has_high = place < 63
    second = lax.broadcasted_iota(jnp.int32, (1, 128), 1) >= 64

    def put(dst, k, value):
        dst[k, PAD : PAD + HALF, :] = value
        dst[k, PAD - 1 : PAD, :] = jnp.where(second, pltpu.roll(value[HALF - 1 :], 64, axis=1), 0.0)
        dst[k, PAD + HALF : PAD + HALF + 1, :] = jnp.where(
            second, 0.0, pltpu.roll(value[:1], 64, axis=1)
        )

    def coefficients(k, carry):
        live = jnp.where(k < 4, not_first, jnp.where(k > 7, not_last, 1.0))
        thick = 1.0 + coef[0, k]
        ratio = live / (6.0 + 0.05 * thick)
        source = 4.0 * coef[1, k] * thick * ratio
        b_ref[k] = ratio
        a_ref[k] = source
        put(x0, k, source)
        return carry

    lax.fori_loop(0, 12, coefficients, 0)
    def sweep(src, dst, start, stop, shift=0):
        def body(i, carry):
            for k in (start + 2 * i, start + 2 * i + 1):
                here = src[k, PAD : PAD + HALF, :]
                total = src[k - 1, PAD : PAD + HALF, :] + src[k + 1, PAD : PAD + HALF, :]
                total += src[k, PAD - 1 : PAD + HALF - 1, :] + src[k, PAD + 1 : PAD + HALF + 1, :]
                total += jnp.where(has_low, pltpu.roll(here, 1, axis=1), 0.0)
                total += jnp.where(has_high, pltpu.roll(here, 127, axis=1), 0.0)
                put(dst, k - shift, a_ref[k] + b_ref[k] * total)
            return carry

        lax.fori_loop(0, (stop - start) // 2, body, 0)

    def exchange(buffer, n):
        src = buffer.at[4:8]
        copies = [
            send(src, buffer.at[0:4], p_send.at[n, 0], p_recv.at[n, 0], at(quad, nexts)),
            send(src, buffer.at[8:12], p_send.at[n, 1], p_recv.at[n, 1], at(quad, prevs)),
        ]
        for copy in copies:
            copy.wait_recv()

        @pl.when(slab == 0)
        def _():
            buffer[0:4] = jnp.zeros((4, HELD, 128), F32)

        @pl.when(slab == slabs - 1)
        def _():
            buffer[8:12] = jnp.zeros((4, HELD, 128), F32)

        return copies

    sweep(x0, x1, 1, 11)
    sweep(x1, x0, 2, 10)
    sweep(x0, x1, 3, 9)
    sweep(x1, y0, 4, 8)
    early = exchange(y0, 0)
    sweep(y0, x0, 1, 11)
    sweep(x0, x1, 2, 10)
    sweep(x1, x0, 3, 9)
    sweep(x0, z0, 4, 8)
    later = exchange(z0, 1)
    sweep(z0, x0, 1, 11)
    sweep(x0, x1, 2, 10)
    sweep(x1, p_ref, 3, 9, shift=3)

    for copies in scatter + gather:
        for copy in copies.values():
            copy.wait_send()
    for copy in halos + early + later:
        copy.wait_send()


def store_split(halves, high_ref, low_ref, f, pair):
    for h, half in enumerate(halves):
        hi, lo = split(half)
        r = f * CB + h * HALF
        high_ref[r : r + HALF, pair * 128 : (pair + 1) * 128] = hi
        low_ref[r : r + HALF, pair * 128 : (pair + 1) * 128] = lo


def sample(cell_ref, weight_ref, high_ref, low_ref, fields, done):
    def one(base):
        tile = pl.ds(base, GTILE)
        rows = one_hot_rows(row_index(cell_ref[:, tile]), GTILE)
        weight = weight_ref[:, tile]
        upper = 1.0 - weight
        along = cell_ref[3:4, tile]
        wanted = lax.broadcasted_iota(jnp.int32, (CB, GTILE), 0)
        pick = jnp.where(wanted == along, weight, jnp.where(wanted == along + 1, upper, 0.0))
        picked = jnp.dot(high_ref[...], rows, preferred_element_type=F32)
        picked += jnp.dot(low_ref[...], rows, preferred_element_type=F32)
        done(
            tile,
            [
                jnp.sum(pick * picked[f * CB : (f + 1) * CB], axis=0, keepdims=True)
                for f in range(fields)
            ],
        )

    def body(i, carry):
        for j in range(UNROLL):
            one(pl.multiple_of((i * UNROLL + j) * GTILE, GTILE))
        return carry

    lax.fori_loop(0, cell_ref.shape[1] // (GTILE * UNROLL), body, 0)


def sample_kernel(
    count_ref,
    cell_ref,
    weight_ref,
    volume_ref,
    velocity_ref,
    p_ref,
    solid_ref,
    pressure_ref,
    drag_ref,
    high_ref,
    low_ref,
    turned,
):
    lane = lax.broadcasted_iota(jnp.int32, (HALF, 128), 1)
    first = lane < 64
    place = lax.rem(lane, 64)
    inner = slice(PAD, PAD + HALF)
    for pair in range(2):
        layers = []
        for k in (2 * pair, 2 * pair + 1):
            here = p_ref[k + 1, inner, :]
            fields = [-0.5 * (p_ref[k + 2, inner, :] - p_ref[k, inner, :])]
            right = jnp.where(place < 63, pltpu.roll(here, 127, axis=1), 0.0)
            left = jnp.where(place > 0, pltpu.roll(here, 1, axis=1), 0.0)
            fields.append(-0.5 * (right - left))
            fields.append(
                -0.5
                * (p_ref[k + 1, PAD + 1 : PAD + HALF + 1, :] - p_ref[k + 1, PAD - 1 : PAD + HALF - 1, :])
            )
            layers.append(fields)
            turned[k] = here.T
        for f in range(3):
            store_split(fold(layers[0][f], layers[1][f], first), high_ref, low_ref, f, pair)
    quad = lax.axis_index("quad")
    for layer in range(CH):
        for h in range(2):
            at = pl.multiple_of(h * 64 + quad * CA, CA)
            pressure_ref[layer, :, h * HALF : (h + 1) * HALF] = turned[layer, pl.ds(at, CA), :]

    def finish(tile, sampled):
        slots = tile.start + lax.broadcasted_iota(jnp.int32, (1, GTILE), 1)
        mass = jnp.where(slots < count_ref[0], volume_ref[:, tile], 0.0)
        factor = mass * (1.0 + solid_ref[:, tile]) ** 2
        for f in range(3):
            drag_ref[f : f + 1, tile] = factor * (sampled[f] - velocity_ref[f : f + 1, tile])

    sample(cell_ref, weight_ref, high_ref, low_ref, 3, finish)


def body(slabs, grain_cell, grain_count, grain_weight, grain_volume, grain_velocity):
    grains = grain_weight.shape[0]
    weight = grain_weight.reshape(1, grains)
    volume = grain_volume.reshape(1, grains)
    smem = pl.BlockSpec(memory_space=pltpu.SMEM)
    vmem = pl.BlockSpec(memory_space=pltpu.VMEM)
    dma = pltpu.SemaphoreType.DMA
    pressure, solid = pl.pallas_call(
        functools.partial(relax_kernel, slabs),
        out_shape=(
            jax.ShapeDtypeStruct((CH + 2, HELD, 128), F32),
            jax.ShapeDtypeStruct((1, grains), F32),
        ),
        in_specs=[smem, vmem, vmem, vmem, vmem],
        out_specs=(vmem, vmem),
        scratch_shapes=[
            pltpu.VMEM((2, CH, HALF, 128), F32),
            pltpu.VMEM((4 * CB, ROWS), F32),
            pltpu.VMEM((4 * CB, GBLOCK), BF16),
            pltpu.VMEM((4 * CB, GBLOCK), BF16),
            pltpu.VMEM((CB, ROWS), BF16),
            pltpu.VMEM((CB, ROWS), BF16),
            pltpu.VMEM((2, 3, CH, CHUNK, 128), F32),
            pltpu.VMEM((2, 3 * CH, HALF, 128), F32),
            pltpu.VMEM((3 * CH, HALF, 128), F32),
            pltpu.VMEM((3 * CH, HALF, 128), F32),
        ]
        + [pltpu.VMEM((3 * CH, HELD, 128), F32)] * 4
        + [dma((2, 3))] * 4
        + [dma((2, 2, QUADS))] * 2
        + [dma((2, 2))] * 2,
        compiler_params=pltpu.CompilerParams(collective_id=0, has_side_effects=True),
        name="relax",
    )(grain_count, grain_cell, weight, volume, grain_velocity)
    return pl.pallas_call(
        sample_kernel,
        out_shape=(
            jax.ShapeDtypeStruct((CH, CA, CB), F32),
            jax.ShapeDtypeStruct((3, grains), F32),
        ),
        in_specs=[smem] + [vmem] * 6,
        out_specs=(vmem, vmem),
        scratch_shapes=[
            pltpu.VMEM((3 * CB, ROWS), BF16),
            pltpu.VMEM((3 * CB, ROWS), BF16),
            pltpu.VMEM((CH, 128, HALF), F32),
        ],
        name="sample",
    )(grain_count, grain_cell, weight, volume, grain_velocity, pressure, solid)


def solution(mesh):
    placed = (
        P(None, ("slab", "quad")),
        P(("slab", "quad")),
        P(("slab", "quad")),
        P(("slab", "quad")),
        P(None, ("slab", "quad")),
    )
    return jax.shard_map(
        functools.partial(body, mesh.shape["slab"]),
        mesh=mesh,
        in_specs=placed,
        out_specs=(P("slab", "quad", None), P(None, ("slab", "quad"))),
        check_vma=False,
    )
```

```python
import functools

import jax
import jax.numpy as jnp
from jax import lax
from jax.experimental import pallas as pl
from jax.experimental.pallas import tpu as pltpu
from jax.sharding import PartitionSpec as P

CH = 4
CA = 16
CB = 256
QUADS = 4
ROWS = CH * CA * QUADS
ACROSS = CA * QUADS
PAD = 8
HALF = CB // 2
HELD = ACROSS + 2 * PAD
GBLOCK = 1024
GTILE = 512
UNROLL = 4

F32 = jnp.float32
BF16 = jnp.bfloat16


def split(x):
    high = x.astype(BF16)
    return high, (x - high.astype(F32)).astype(BF16)


def row_index(cell):
    return cell[1:2] * ACROSS + cell[0:1] * CA + cell[2:3]


def small(x):
    return x.astype(F32).astype(BF16)


def one_hot_rows(rows, width):
    wanted = small(lax.broadcasted_iota(jnp.int32, (ROWS, width), 0))
    return jnp.where(wanted == small(rows), BF16(1.0), BF16(0.0))


def masses(count_ref, vol, start, width):
    slots = start + lax.broadcasted_iota(jnp.int32, (1, width), 1)
    return jnp.where(slots < count_ref[0], vol, 0.0)


def keys(cell):
    along = cell[3:4]
    above = along + 1

    def key(x):
        return (x & 1) * HALF + (x >> 1)

    return key(along), key(above)


def deposit(field, count_ref, cell_ref, weight_ref, volume_ref, velocity_ref, out_ref, total, va, vb):
    total[...] = jnp.zeros_like(total)
    blocks = cell_ref.shape[1] // GBLOCK

    def tile_of(t):
        return pl.ds(pl.multiple_of(t * GBLOCK, GBLOCK), GBLOCK)

    def build(t, spread):
        tile = tile_of(t)
        weight = weight_ref[:, tile]
        amount = masses(count_ref, volume_ref[:, tile], t * GBLOCK, GBLOCK)
        if field:
            amount = amount * velocity_ref[0:1, tile]
        along, above = (small(x) for x in keys(cell_ref[:, tile]))
        shares = list(zip(split(amount * weight), split(amount * (1.0 - weight))))
        for r in range(0, CB, 16):
            wanted = small(lax.broadcasted_iota(jnp.int32, (16, GBLOCK), 0) + r)
            lower_hit = wanted == along
            upper_hit = wanted == above
            for n, (low, up) in enumerate(shares):
                spread[n * CB + r : n * CB + r + 16, :] = jnp.where(
                    lower_hit, low, jnp.where(upper_hit, up, BF16(0.0))
                )

    def add(t, spread):
        rows = one_hot_rows(row_index(cell_ref[:, tile_of(t)]), GBLOCK)
        total[...] += lax.dot_general(
            spread[...], rows, (((1,), (1,)), ((), ())), preferred_element_type=F32
        )

    build(0, va)

    def body(i, carry):
        t = 2 * i
        build(t + 1, vb)
        add(t, va)
        build(jnp.minimum(t + 2, blocks - 1), va)
        add(t + 1, vb)
        return carry

    lax.fori_loop(0, blocks // 2, body, 0)
    for pair in range(2):
        lanes = slice(pair * 128, (pair + 1) * 128)
        whole = total[:CB, lanes] + total[CB:, lanes]
        for odd in range(2):
            block = whole[odd * HALF : (odd + 1) * HALF].T
            for j in range(2):
                out_ref[field, 2 * pair + j, odd] = block[j * ACROSS : (j + 1) * ACROSS]


def relax_kernel(
    slabs,
    count_ref,
    cell_ref,
    weight_ref,
    volume_ref,
    velocity_ref,
    p_ref,
    solid_ref,
    d_ref,
    total_ref,
    va,
    vb,
    terms_ref,
    gathered,
    coef,
    a_ref,
    b_ref,
    x0,
    x1,
    y0,
    z0,
    rs_send,
    rs_recv,
    ag_send,
    ag_recv,
    halo_send,
    halo_recv,
    p_send,
    p_recv,
):
    quad = lax.axis_index("quad")
    slab = lax.axis_index("slab")
    nexts = lax.rem(slab + 1, slabs)
    prevs = lax.rem(slab + slabs - 1, slabs)
    peers = [lax.rem(quad + d, QUADS) for d in range(QUADS)]
    origins = [lax.rem(quad + QUADS - d, QUADS) for d in range(QUADS)]

    def at(q, s):
        return {"quad": q, "slab": s}

    def rows_of(q):
        return pl.ds(pl.multiple_of(q * CA, CA), CA)

    barrier = pltpu.get_barrier_semaphore()
    has_prev = slab > 0
    has_next = slab < slabs - 1

    def greet(where):
        pl.semaphore_signal(
            barrier, inc=1, device_id=where, device_id_type=pl.DeviceIdType.MESH
        )

    for d in range(1, QUADS):
        greet(at(peers[d], slab))

    @pl.when(has_next)
    def _():
        greet(at(quad, nexts))

    @pl.when(has_prev)
    def _():
        greet(at(quad, prevs))

    for buffer in (x0, x1, y0, z0, p_ref):
        rim = jnp.zeros((buffer.shape[0], 2, PAD, 128), F32)
        buffer[:, :, :PAD, :] = rim
        buffer[:, :, PAD + ACROSS :, :] = rim

    @pl.when(slab == 0)
    def _():
        for field in range(2):
            coef[field, 0:4] = jnp.zeros((4, 2, ACROSS, 128), F32)
        for buffer in (y0, z0):
            buffer[0:4] = jnp.zeros((4, 2, HELD, 128), F32)

    @pl.when(slab == slabs - 1)
    def _():
        for field in range(2):
            coef[field, 8:12] = jnp.zeros((4, 2, ACROSS, 128), F32)
        for buffer in (y0, z0):
            buffer[8:12] = jnp.zeros((4, 2, HELD, 128), F32)

    def link(src, dst, ssem, rsem, where):
        return pltpu.make_async_remote_copy(
            src_ref=src,
            dst_ref=dst,
            send_sem=ssem,
            recv_sem=rsem,
            device_id=where,
            device_id_type=pl.DeviceIdType.MESH,
        )

    def send(*args):
        copy = link(*args)
        copy.start()
        return copy

    def each_side(copies, up, down):
        @pl.when(has_next)
        def _():
            up(copies[0])

        @pl.when(has_prev)
        def _():
            down(copies[1])

    def start(copies):
        each_side(copies, lambda c: c.start(), lambda c: c.start())

    def sent(copies):
        each_side(copies, lambda c: c.wait_send(), lambda c: c.wait_send())

    def arrived(copies):
        each_side(copies[::-1], lambda c: c.wait_recv(), lambda c: c.wait_recv())

    scatter, gather, halos = [], [], []
    for f in range(2):
        deposit(f, count_ref, cell_ref, weight_ref, volume_ref, velocity_ref, d_ref, total_ref, va, vb)
        if f == 0:
            callers = QUADS - 1 + has_prev.astype(jnp.int32) + has_next.astype(jnp.int32)
            pl.semaphore_wait(barrier, callers)
        scatter.append(
            {
                d: send(
                    d_ref.at[f, :, :, rows_of(peers[d]), :],
                    gathered.at[f, d - 1],
                    rs_send.at[f, d - 1],
                    rs_recv.at[f, d - 1],
                    at(peers[d], slab),
                )
                for d in (2, 1, 3)
            }
        )
    own = rows_of(quad)

    def forward(f, d):
        block = rows_of(origins[d])
        src = coef.at[f, 4:8, :, block, :]
        pair = [
            link(
                src,
                coef.at[f, low : low + 4, :, block, :],
                halo_send.at[f, side, d],
                halo_recv.at[f, side, d],
                at(quad, where),
            )
            for side, (low, where) in enumerate(((0, nexts), (8, prevs)))
        ]
        start(pair)
        halos.append(pair)

    for f in range(2):
        for copy in scatter[f].values():
            copy.wait_recv()
        coef[f, 4:8, :, own, :] = (d_ref[f, :, :, own, :] + gathered[f, 0]) + (
            gathered[f, 1] + gathered[f, 2]
        )
        mine = coef.at[f, 4:8, :, own, :]
        gather.append(
            {
                d: send(mine, mine, ag_send.at[f, d - 1], ag_recv.at[f, d - 1], at(peers[d], slab))
                for d in (2, 1, 3)
            }
        )
        forward(f, 0)
    for f in range(2):
        for d in (1, 3, 2):
            gather[f][d].wait_recv()
            forward(f, d)

    for pair in halos:
        arrived(pair)


    lane = lax.broadcasted_iota(jnp.int32, (ACROSS, 128), 1)
    inner = slice(PAD, PAD + ACROSS)

    def coefficients(k, carry):
        inside = jnp.logical_and(
            jnp.logical_or(k >= 4, has_prev), jnp.logical_or(k <= 7, has_next)
        )
        thick = 1.0 + coef[0, k]
        ratio = jnp.where(inside, 1.0, 0.0) / (6.0 + 0.05 * thick)
        source = 4.0 * coef[1, k] * thick * ratio
        b_ref[k] = ratio
        a_ref[k] = source
        x0[k, :, inner, :] = source
        return carry

    lax.fori_loop(0, 12, coefficients, 0)
    def sweep(src, dst, begin, end, shift=0):
        half = (end - begin) // 2

        def body(i, carry):
            for j in range(half):
                k = begin + half * i + j
                for odd in range(2):
                    other = src[k, 1 - odd, inner, :]
                    if odd:
                        turned = jnp.where(lane < 127, pltpu.roll(other, 127, axis=1), 0.0)
                    else:
                        turned = jnp.where(lane > 0, pltpu.roll(other, 1, axis=1), 0.0)
                    total = src[k - 1, odd, inner, :] + src[k + 1, odd, inner, :]
                    total += src[k, odd, PAD - 1 : PAD + ACROSS - 1, :]
                    total += src[k, odd, PAD + 1 : PAD + ACROSS + 1, :]
                    total += other + turned
                    dst[k - shift, odd, inner, :] = a_ref[k, odd] + b_ref[k, odd] * total
            return carry

        lax.fori_loop(0, 2, body, 0)

    def exchange(buffer, n):
        def block(low):
            return buffer.at[low : low + 4, :, PAD : PAD + ACROSS, :]

        src = block(4)
        pair = [
            link(src, block(0), p_send.at[n, 0], p_recv.at[n, 0], at(quad, nexts)),
            link(src, block(8), p_send.at[n, 1], p_recv.at[n, 1], at(quad, prevs)),
        ]
        start(pair)
        return pair

    sweep(x0, x1, 1, 11)
    sweep(x1, x0, 2, 10)
    sweep(x0, x1, 3, 9)
    sweep(x1, y0, 4, 8)
    early = exchange(y0, 0)
    for pair in range(2):
        for odd in range(2):
            block = [coef[0, 4 + 2 * pair + j, odd] for j in range(2)]
            store_split(block, terms_ref, 0, 1, pair, odd)

    def keep(tile, sampled):
        solid_ref[:, tile] = sampled[0]

    sample(cell_ref, weight_ref, terms_ref, 1, keep)
    arrived(early)
    sweep(y0, x0, 1, 11)
    sweep(x0, x1, 2, 10)
    sweep(x1, x0, 3, 9)
    sweep(x0, z0, 4, 8)
    later = exchange(z0, 1)
    arrived(later)
    sweep(z0, x0, 1, 11)
    sweep(x0, x1, 2, 10)
    sweep(x1, p_ref, 3, 9, shift=3)

    for copies in scatter + gather:
        for copy in copies.values():
            copy.wait_send()
    for pair in halos + [early, later]:
        sent(pair)


def store_split(blocks, terms_ref, f, fields, pair, odd):
    hi, lo = split(jnp.concatenate(blocks, axis=0).T)
    r = f * CB + odd * HALF
    lanes = slice(pair * 128, (pair + 1) * 128)
    terms_ref[r : r + HALF, lanes] = hi
    terms_ref[r + fields * CB : r + fields * CB + HALF, lanes] = lo


def sample(cell_ref, weight_ref, terms_ref, fields, done):
    def one(base):
        tile = pl.ds(base, GTILE)
        rows = one_hot_rows(row_index(cell_ref[:, tile]), GTILE)
        weight = weight_ref[:, tile]
        upper = 1.0 - weight
        along, above = keys(cell_ref[:, tile])
        wanted = lax.broadcasted_iota(jnp.int32, (CB, GTILE), 0)
        pick = jnp.where(wanted == along, weight, jnp.where(wanted == above, upper, 0.0))
        both = jnp.dot(terms_ref[...], rows, preferred_element_type=F32)
        picked = both[: fields * CB] + both[fields * CB :]
        done(
            tile,
            [
                jnp.sum(pick * picked[f * CB : (f + 1) * CB], axis=0, keepdims=True)
                for f in range(fields)
            ],
        )

    def body(i, carry):
        for j in range(UNROLL):
            one(pl.multiple_of((i * UNROLL + j) * GTILE, GTILE))
        return carry

    lax.fori_loop(0, cell_ref.shape[1] // (GTILE * UNROLL), body, 0)


def sample_kernel(
    count_ref,
    cell_ref,
    weight_ref,
    volume_ref,
    velocity_ref,
    p_ref,
    solid_ref,
    pressure_ref,
    drag_ref,
    terms_ref,
    turned,
):
    lane = lax.broadcasted_iota(jnp.int32, (ACROSS, 128), 1)
    inner = slice(PAD, PAD + ACROSS)
    for pair in range(2):
        for odd in range(2):
            blocks = [[], [], []]
            for k in (2 * pair + 1, 2 * pair + 2):
                other = p_ref[k, 1 - odd, inner, :]
                if odd:
                    right, left = jnp.where(lane < 127, pltpu.roll(other, 127, axis=1), 0.0), other
                else:
                    right, left = other, jnp.where(lane > 0, pltpu.roll(other, 1, axis=1), 0.0)
                blocks[0].append(-0.5 * (p_ref[k + 1, odd, inner, :] - p_ref[k - 1, odd, inner, :]))
                blocks[1].append(
                    -0.5
                    * (
                        p_ref[k, odd, PAD + 1 : PAD + ACROSS + 1, :]
                        - p_ref[k, odd, PAD - 1 : PAD + ACROSS - 1, :]
                    )
                )
                blocks[2].append(-0.5 * (right - left))
            for f in range(3):
                store_split(blocks[f], terms_ref, f, 3, pair, odd)
    quad = lax.axis_index("quad")
    mine = pl.ds(pl.multiple_of(PAD + quad * CA, PAD), CA)
    swapped = jnp.concatenate(
        [p_ref[k + 1, odd, mine, :] for odd in range(2) for k in range(CH)], axis=0
    ).T
    turned[pl.ds(0, HALF, stride=2), :] = swapped
    turned[pl.ds(1, HALF, stride=2), :] = pltpu.roll(swapped, 64, axis=1)
    whole = turned[...].T
    for k in range(CH):
        pressure_ref[k] = whole[k * CA : (k + 1) * CA]

    def finish(tile, sampled):
        slots = tile.start + lax.broadcasted_iota(jnp.int32, (1, GTILE), 1)
        mass = jnp.where(slots < count_ref[0], volume_ref[:, tile], 0.0)
        factor = mass * (1.0 + solid_ref[:, tile]) ** 2
        for f in range(3):
            drag_ref[f : f + 1, tile] = factor * (sampled[f] - velocity_ref[f : f + 1, tile])

    sample(cell_ref, weight_ref, terms_ref, 3, finish)


def body(slabs, grain_cell, grain_count, grain_weight, grain_volume, grain_velocity):
    grains = grain_weight.shape[0]
    weight = grain_weight.reshape(1, grains)
    volume = grain_volume.reshape(1, grains)
    smem = pl.BlockSpec(memory_space=pltpu.SMEM)
    vmem = pl.BlockSpec(memory_space=pltpu.VMEM)
    dma = pltpu.SemaphoreType.DMA
    pressure, solid = pl.pallas_call(
        functools.partial(relax_kernel, slabs),
        out_shape=(
            jax.ShapeDtypeStruct((CH + 2, 2, HELD, 128), F32),
            jax.ShapeDtypeStruct((1, grains), F32),
        ),
        in_specs=[smem, vmem, vmem, vmem, vmem],
        out_specs=(vmem, vmem),
        scratch_shapes=[
            pltpu.VMEM((2, CH, 2, ACROSS, 128), F32),
            pltpu.VMEM((2 * CB, ROWS), F32),
            pltpu.VMEM((2 * CB, GBLOCK), BF16),
            pltpu.VMEM((2 * CB, GBLOCK), BF16),
            pltpu.VMEM((2 * CB, ROWS), BF16),
            pltpu.VMEM((2, 3, CH, 2, CA, 128), F32),
            pltpu.VMEM((2, 3 * CH, 2, ACROSS, 128), F32),
            pltpu.VMEM((3 * CH, 2, ACROSS, 128), F32),
            pltpu.VMEM((3 * CH, 2, ACROSS, 128), F32),
        ]
        + [pltpu.VMEM((3 * CH, 2, HELD, 128), F32)] * 4
        + [dma((2, 3))] * 4
        + [dma((2, 2, QUADS))] * 2
        + [dma((2, 2))] * 2,
        compiler_params=pltpu.CompilerParams(collective_id=0, has_side_effects=True),
        name="relax",
    )(grain_count, grain_cell, weight, volume, grain_velocity)
    return pl.pallas_call(
        sample_kernel,
        out_shape=(
            jax.ShapeDtypeStruct((CH, CA, CB), F32),
            jax.ShapeDtypeStruct((3, grains), F32),
        ),
        in_specs=[smem] + [vmem] * 6,
        out_specs=(vmem, vmem),
        scratch_shapes=[
            pltpu.VMEM((6 * CB, ROWS), BF16),
            pltpu.VMEM((CB, 128), F32),
        ],
        name="sample",
    )(grain_count, grain_cell, weight, volume, grain_velocity, pressure, solid)


def solution(mesh):
    placed = (
        P(None, ("slab", "quad")),
        P(("slab", "quad")),
        P(("slab", "quad")),
        P(("slab", "quad")),
        P(None, ("slab", "quad")),
    )
    return jax.shard_map(
        functools.partial(body, mesh.shape["slab"]),
        mesh=mesh,
        in_specs=placed,
        out_specs=(P("slab", "quad", None), P(None, ("slab", "quad"))),
        check_vma=False,
    )
```

```python
import functools

import jax
import jax.numpy as jnp
from jax import lax
from jax.experimental import pallas as pl
from jax.experimental.pallas import tpu as pltpu
from jax.sharding import PartitionSpec as P

CH = 4
CA = 16
CB = 256
QUADS = 4
ROWS = CH * CA * QUADS
ACROSS = CA * QUADS
PAD = 8
HALF = CB // 2
HELD = ACROSS + 2 * PAD
GBLOCK = 1024
GTILE = 512
UNROLL = 16

F32 = jnp.float32
BF16 = jnp.bfloat16


def split(x):
    high = x.astype(BF16)
    return high, (x - high.astype(F32)).astype(BF16)


def row_index(cell):
    return cell[1:2] * ACROSS + cell[0:1] * CA + cell[2:3]


def small(x):
    return x.astype(F32).astype(BF16)


def one_hot_rows(rows, width):
    wanted = small(lax.broadcasted_iota(jnp.int32, (ROWS, width), 0))
    return jnp.where(wanted == small(rows), BF16(1.0), BF16(0.0))


def masses(count_ref, vol, start, width):
    slots = start + lax.broadcasted_iota(jnp.int32, (1, width), 1)
    return jnp.where(slots < count_ref[0], vol, 0.0)


def keys(cell):
    along = cell[3:4]
    above = along + 1

    def key(x):
        return (x & 1) * HALF + (x >> 1)

    return key(along), key(above)


def deposit(field, count_ref, cell_ref, weight_ref, volume_ref, velocity_ref, out_ref, total_ref, va, vb):
    blocks = cell_ref.shape[1] // GBLOCK

    def tile_of(t):
        return slice(t * GBLOCK, (t + 1) * GBLOCK)

    def build(t, spread):
        tile = tile_of(t)
        weight = weight_ref[:, tile]
        amount = masses(count_ref, volume_ref[:, tile], t * GBLOCK, GBLOCK)
        if field:
            amount = amount * velocity_ref[0:1, tile]
        along, above = (small(x) for x in keys(cell_ref[:, tile]))
        shares = list(zip(split(amount * weight), split(amount * (1.0 - weight))))
        for r in range(0, CB, 16):
            wanted = small(lax.broadcasted_iota(jnp.int32, (16, GBLOCK), 0) + r)
            lower_hit = wanted == along
            upper_hit = wanted == above
            for n, (low, up) in enumerate(shares):
                spread[n * CB + r : n * CB + r + 16, :] = jnp.where(
                    lower_hit, low, jnp.where(upper_hit, up, BF16(0.0))
                )

    def product(t, spread):
        rows = one_hot_rows(row_index(cell_ref[:, tile_of(t)]), GBLOCK)
        return lax.dot_general(
            rows, spread[...], (((1,), (1,)), ((), ())), preferred_element_type=F32
        )

    total = None
    slots = (va, vb)
    build(0, va)
    for t in range(blocks):
        if t + 1 < blocks:
            build(t + 1, slots[(t + 1) % 2])
        part = product(t, slots[t % 2])
        total = part if total is None else total + part
    total_ref[...] = total

    def settle(layer, carry):
        here = pl.ds(pl.multiple_of(layer * ACROSS, ACROSS), ACROSS)
        for odd in range(2):
            out_ref[field, layer, odd] = (
                total_ref[here, odd * HALF : (odd + 1) * HALF]
                + total_ref[here, CB + odd * HALF : CB + (odd + 1) * HALF]
            )
        return carry

    lax.fori_loop(0, CH, settle, 0)


def relax_kernel(
    slabs,
    count_ref,
    cell_ref,
    weight_ref,
    volume_ref,
    velocity_ref,
    p_ref,
    solid_ref,
    d_ref,
    total_ref,
    va,
    vb,
    terms_ref,
    gathered,
    coef,
    a_ref,
    b_ref,
    x0,
    x1,
    y0,
    z0,
    rs_send,
    rs_recv,
    ag_send,
    ag_recv,
    halo_send,
    halo_recv,
    p_send,
    p_recv,
):
    quad = lax.axis_index("quad")
    slab = lax.axis_index("slab")
    nexts = lax.rem(slab + 1, slabs)
    prevs = lax.rem(slab + slabs - 1, slabs)
    peers = [lax.rem(quad + d, QUADS) for d in range(QUADS)]
    origins = [lax.rem(quad + QUADS - d, QUADS) for d in range(QUADS)]

    def at(q, s):
        return {"quad": q, "slab": s}

    def rows_of(q):
        return pl.ds(pl.multiple_of(q * CA, CA), CA)

    barrier = pltpu.get_barrier_semaphore()
    has_prev = slab > 0
    has_next = slab < slabs - 1

    def greet(where):
        pl.semaphore_signal(
            barrier, inc=1, device_id=where, device_id_type=pl.DeviceIdType.MESH
        )

    for d in range(1, QUADS):
        greet(at(peers[d], slab))

    @pl.when(has_next)
    def _():
        greet(at(quad, nexts))

    @pl.when(has_prev)
    def _():
        greet(at(quad, prevs))

    def link(src, dst, ssem, rsem, where):
        return pltpu.make_async_remote_copy(
            src_ref=src,
            dst_ref=dst,
            send_sem=ssem,
            recv_sem=rsem,
            device_id=where,
            device_id_type=pl.DeviceIdType.MESH,
        )

    def send(*args):
        copy = link(*args)
        copy.start()
        return copy

    def each_side(copies, up, down):
        @pl.when(has_next)
        def _():
            up(copies[0])

        @pl.when(has_prev)
        def _():
            down(copies[1])

    def start(copies):
        each_side(copies, lambda c: c.start(), lambda c: c.start())

    def sent(copies):
        each_side(copies, lambda c: c.wait_send(), lambda c: c.wait_send())

    def arrived(copies):
        each_side(copies[::-1], lambda c: c.wait_recv(), lambda c: c.wait_recv())

    scatter, gather, halos = [], [], []
    for f in range(2):
        deposit(f, count_ref, cell_ref, weight_ref, volume_ref, velocity_ref, d_ref, total_ref, va, vb)
        if f == 0:
            callers = QUADS - 1 + has_prev.astype(jnp.int32) + has_next.astype(jnp.int32)
            pl.semaphore_wait(barrier, callers)
        scatter.append(
            {
                d: send(
                    d_ref.at[f, :, :, rows_of(peers[d]), :],
                    gathered.at[f, d - 1],
                    rs_send.at[f, d - 1],
                    rs_recv.at[f, d - 1],
                    at(peers[d], slab),
                )
                for d in (2, 1, 3)
            }
        )
    for buffer in (x0, x1, y0, z0, p_ref):
        rim = jnp.zeros((buffer.shape[0], 2, PAD, 128), F32)
        buffer[:, :, :PAD, :] = rim
        buffer[:, :, PAD + ACROSS :, :] = rim

    @pl.when(slab == 0)
    def _():
        for field in range(2):
            coef[field, 0:4] = jnp.zeros((4, 2, ACROSS, 128), F32)
        for buffer in (y0, z0):
            buffer[0:4] = jnp.zeros((4, 2, HELD, 128), F32)

    @pl.when(slab == slabs - 1)
    def _():
        for field in range(2):
            coef[field, 8:12] = jnp.zeros((4, 2, ACROSS, 128), F32)
        for buffer in (y0, z0):
            buffer[8:12] = jnp.zeros((4, 2, HELD, 128), F32)

    own = rows_of(quad)

    def forward(f, d):
        block = rows_of(origins[d])
        src = coef.at[f, 4:8, :, block, :]
        pair = [
            link(
                src,
                coef.at[f, low : low + 4, :, block, :],
                halo_send.at[f, side, d],
                halo_recv.at[f, side, d],
                at(quad, where),
            )
            for side, (low, where) in enumerate(((0, nexts), (8, prevs)))
        ]
        start(pair)
        halos.append(pair)

    for f in range(2):
        for copy in scatter[f].values():
            copy.wait_recv()
        coef[f, 4:8, :, own, :] = (d_ref[f, :, :, own, :] + gathered[f, 0]) + (
            gathered[f, 1] + gathered[f, 2]
        )
        mine = coef.at[f, 4:8, :, own, :]
        gather.append(
            {
                d: send(mine, mine, ag_send.at[f, d - 1], ag_recv.at[f, d - 1], at(peers[d], slab))
                for d in (2, 1, 3)
            }
        )
        forward(f, 0)
    for f in range(2):
        for d in (1, 3, 2):
            gather[f][d].wait_recv()
            forward(f, d)

    for pair in halos:
        arrived(pair)


    lane = lax.broadcasted_iota(jnp.int32, (ACROSS, 128), 1)
    inner = slice(PAD, PAD + ACROSS)

    def coefficients(k, carry):
        inside = jnp.logical_and(
            jnp.logical_or(k >= 4, has_prev), jnp.logical_or(k <= 7, has_next)
        )
        thick = 1.0 + coef[0, k]
        ratio = jnp.where(inside, 1.0, 0.0) / (6.0 + 0.05 * thick)
        source = 4.0 * coef[1, k] * thick * ratio
        b_ref[k] = ratio
        a_ref[k] = source
        x0[k, :, inner, :] = source
        return carry

    lax.fori_loop(0, 12, coefficients, 0)
    def sweep(src, dst, begin, end, shift=0):
        half = (end - begin) // 2

        def body(i, carry):
            for j in range(half):
                k = begin + half * i + j
                for odd in range(2):
                    other = src[k, 1 - odd, inner, :]
                    if odd:
                        turned = jnp.where(lane < 127, pltpu.roll(other, 127, axis=1), 0.0)
                    else:
                        turned = jnp.where(lane > 0, pltpu.roll(other, 1, axis=1), 0.0)
                    total = src[k - 1, odd, inner, :] + src[k + 1, odd, inner, :]
                    total += src[k, odd, PAD - 1 : PAD + ACROSS - 1, :]
                    total += src[k, odd, PAD + 1 : PAD + ACROSS + 1, :]
                    total += other + turned
                    dst[k - shift, odd, inner, :] = a_ref[k, odd] + b_ref[k, odd] * total
            return carry

        lax.fori_loop(0, 2, body, 0)

    def exchange(buffer, n):
        def block(low):
            return buffer.at[low : low + 4, :, PAD : PAD + ACROSS, :]

        src = block(4)
        pair = [
            link(src, block(0), p_send.at[n, 0], p_recv.at[n, 0], at(quad, nexts)),
            link(src, block(8), p_send.at[n, 1], p_recv.at[n, 1], at(quad, prevs)),
        ]
        start(pair)
        return pair

    sweep(x0, x1, 1, 11)
    sweep(x1, x0, 2, 10)
    sweep(x0, x1, 3, 9)
    sweep(x1, y0, 4, 8)
    early = exchange(y0, 0)
    for pair in range(2):
        for odd in range(2):
            block = [coef[0, 4 + 2 * pair + j, odd] for j in range(2)]
            store_split(block, terms_ref, 0, 1, pair, odd)

    def keep(tile, sampled):
        solid_ref[:, tile] = sampled[0]

    sample(cell_ref, weight_ref, terms_ref, 1, keep)
    arrived(early)
    sweep(y0, x0, 1, 11)
    sweep(x0, x1, 2, 10)
    sweep(x1, x0, 3, 9)
    sweep(x0, z0, 4, 8)
    later = exchange(z0, 1)
    arrived(later)
    sweep(z0, x0, 1, 11)
    sweep(x0, x1, 2, 10)
    sweep(x1, p_ref, 3, 9, shift=3)

    for copies in scatter + gather:
        for copy in copies.values():
            copy.wait_send()
    for pair in halos + [early, later]:
        sent(pair)


def store_split(blocks, terms_ref, f, fields, pair, odd):
    hi, lo = split(jnp.concatenate(blocks, axis=0).T)
    r = f * CB + odd * HALF
    lanes = slice(pair * 128, (pair + 1) * 128)
    terms_ref[r : r + HALF, lanes] = hi
    terms_ref[r + fields * CB : r + fields * CB + HALF, lanes] = lo


def sample(cell_ref, weight_ref, terms_ref, fields, done):
    def one(base):
        tile = pl.ds(base, GTILE)
        rows = one_hot_rows(row_index(cell_ref[:, tile]), GTILE)
        weight = weight_ref[:, tile]
        upper = 1.0 - weight
        along, above = keys(cell_ref[:, tile])
        wanted = lax.broadcasted_iota(jnp.int32, (CB, GTILE), 0)
        pick = jnp.where(wanted == along, weight, jnp.where(wanted == above, upper, 0.0))
        both = jnp.dot(terms_ref[...], rows, preferred_element_type=F32)
        picked = both[: fields * CB] + both[fields * CB :]
        done(
            tile,
            [
                jnp.sum(pick * picked[f * CB : (f + 1) * CB], axis=0, keepdims=True)
                for f in range(fields)
            ],
        )

    def body(i, carry):
        for j in range(UNROLL):
            one(pl.multiple_of((i * UNROLL + j) * GTILE, GTILE))
        return carry

    lax.fori_loop(0, cell_ref.shape[1] // (GTILE * UNROLL), body, 0)


def sample_kernel(
    count_ref,
    cell_ref,
    weight_ref,
    volume_ref,
    velocity_ref,
    p_ref,
    solid_ref,
    pressure_ref,
    drag_ref,
    terms_ref,
    turned,
):
    lane = lax.broadcasted_iota(jnp.int32, (ACROSS, 128), 1)
    inner = slice(PAD, PAD + ACROSS)
    for pair in range(2):
        for odd in range(2):
            blocks = [[], [], []]
            for k in (2 * pair + 1, 2 * pair + 2):
                other = p_ref[k, 1 - odd, inner, :]
                if odd:
                    right, left = jnp.where(lane < 127, pltpu.roll(other, 127, axis=1), 0.0), other
                else:
                    right, left = other, jnp.where(lane > 0, pltpu.roll(other, 1, axis=1), 0.0)
                blocks[0].append(-0.5 * (p_ref[k + 1, odd, inner, :] - p_ref[k - 1, odd, inner, :]))
                blocks[1].append(
                    -0.5
                    * (
                        p_ref[k, odd, PAD + 1 : PAD + ACROSS + 1, :]
                        - p_ref[k, odd, PAD - 1 : PAD + ACROSS - 1, :]
                    )
                )
                blocks[2].append(-0.5 * (right - left))
            for f in range(3):
                store_split(blocks[f], terms_ref, f, 3, pair, odd)
    quad = lax.axis_index("quad")
    mine = pl.ds(pl.multiple_of(PAD + quad * CA, PAD), CA)
    swapped = jnp.concatenate(
        [p_ref[k + 1, odd, mine, :] for odd in range(2) for k in range(CH)], axis=0
    ).T
    turned[pl.ds(0, HALF, stride=2), :] = swapped
    turned[pl.ds(1, HALF, stride=2), :] = pltpu.roll(swapped, 64, axis=1)
    whole = turned[...].T
    for k in range(CH):
        pressure_ref[k] = whole[k * CA : (k + 1) * CA]

    def finish(tile, sampled):
        slots = tile.start + lax.broadcasted_iota(jnp.int32, (1, GTILE), 1)
        mass = jnp.where(slots < count_ref[0], volume_ref[:, tile], 0.0)
        factor = mass * (1.0 + solid_ref[:, tile]) ** 2
        for f in range(3):
            drag_ref[f : f + 1, tile] = factor * (sampled[f] - velocity_ref[f : f + 1, tile])

    sample(cell_ref, weight_ref, terms_ref, 3, finish)


def body(slabs, grain_cell, grain_count, grain_weight, grain_volume, grain_velocity):
    grains = grain_weight.shape[0]
    weight = grain_weight.reshape(1, grains)
    volume = grain_volume.reshape(1, grains)
    smem = pl.BlockSpec(memory_space=pltpu.SMEM)
    vmem = pl.BlockSpec(memory_space=pltpu.VMEM)
    dma = pltpu.SemaphoreType.DMA
    pressure, solid = pl.pallas_call(
        functools.partial(relax_kernel, slabs),
        out_shape=(
            jax.ShapeDtypeStruct((CH + 2, 2, HELD, 128), F32),
            jax.ShapeDtypeStruct((1, grains), F32),
        ),
        in_specs=[smem, vmem, vmem, vmem, vmem],
        out_specs=(vmem, vmem),
        scratch_shapes=[
            pltpu.VMEM((2, CH, 2, ACROSS, 128), F32),
            pltpu.VMEM((ROWS, 2 * CB), F32),
            pltpu.VMEM((2 * CB, GBLOCK), BF16),
            pltpu.VMEM((2 * CB, GBLOCK), BF16),
            pltpu.VMEM((2 * CB, ROWS), BF16),
            pltpu.VMEM((2, 3, CH, 2, CA, 128), F32),
            pltpu.VMEM((2, 3 * CH, 2, ACROSS, 128), F32),
            pltpu.VMEM((3 * CH, 2, ACROSS, 128), F32),
            pltpu.VMEM((3 * CH, 2, ACROSS, 128), F32),
        ]
        + [pltpu.VMEM((3 * CH, 2, HELD, 128), F32)] * 4
        + [dma((2, 3))] * 4
        + [dma((2, 2, QUADS))] * 2
        + [dma((2, 2))] * 2,
        compiler_params=pltpu.CompilerParams(collective_id=0, has_side_effects=True),
        name="relax",
    )(grain_count, grain_cell, weight, volume, grain_velocity)
    return pl.pallas_call(
        sample_kernel,
        out_shape=(
            jax.ShapeDtypeStruct((CH, CA, CB), F32),
            jax.ShapeDtypeStruct((3, grains), F32),
        ),
        in_specs=[smem] + [vmem] * 6,
        out_specs=(vmem, vmem),
        scratch_shapes=[
            pltpu.VMEM((6 * CB, ROWS), BF16),
            pltpu.VMEM((CB, 128), F32),
        ],
        name="sample",
    )(grain_count, grain_cell, weight, volume, grain_velocity, pressure, solid)


def solution(mesh):
    placed = (
        P(None, ("slab", "quad")),
        P(("slab", "quad")),
        P(("slab", "quad")),
        P(("slab", "quad")),
        P(None, ("slab", "quad")),
    )
    return jax.shard_map(
        functools.partial(body, mesh.shape["slab"]),
        mesh=mesh,
        in_specs=placed,
        out_specs=(P("slab", "quad", None), P(None, ("slab", "quad"))),
        check_vma=False,
    )
```

```python
import functools

import jax
import jax.numpy as jnp
from jax import lax
from jax.experimental import pallas as pl
from jax.experimental.pallas import tpu as pltpu
from jax.sharding import PartitionSpec as P

CH = 4
CA = 16
CB = 256
QUADS = 4
ROWS = CH * CA * QUADS
ACROSS = CA * QUADS
PAD = 8
HALF = CB // 2
HELD = ACROSS + 2 * PAD
GBLOCK = 1024
GTILE = 512
UNROLL = 16

F32 = jnp.float32
BF16 = jnp.bfloat16


def split(x):
    high = x.astype(BF16)
    return high, (x - high.astype(F32)).astype(BF16)


def row_index(cell):
    return cell[1:2] * ACROSS + cell[0:1] * CA + cell[2:3]


def small(x):
    return x.astype(F32).astype(BF16)


def one_hot_rows(rows, width):
    wanted = small(lax.broadcasted_iota(jnp.int32, (ROWS, width), 0))
    return jnp.where(wanted == small(rows), BF16(1.0), BF16(0.0))


def masses(count_ref, vol, start, width):
    slots = start + lax.broadcasted_iota(jnp.int32, (1, width), 1)
    return jnp.where(slots < count_ref[...], vol, 0.0)


def keys(cell):
    along = cell[3:4]
    above = along + 1

    def key(x):
        return (x & 1) * HALF + (x >> 1)

    return key(along), key(above)


def deposit(field, count_ref, cell_ref, weight_ref, volume_ref, velocity_ref, out_ref, total_ref, va, vb):
    blocks = cell_ref.shape[1] // GBLOCK

    def tile_of(t):
        return slice(t * GBLOCK, (t + 1) * GBLOCK)

    def build(t, spread):
        tile = tile_of(t)
        weight = weight_ref[:, tile]
        amount = masses(count_ref, volume_ref[:, tile], t * GBLOCK, GBLOCK)
        if field:
            amount = amount * velocity_ref[0:1, tile]
        along, above = (small(x) for x in keys(cell_ref[:, tile]))
        shares = list(zip(split(amount * weight), split(amount * (1.0 - weight))))
        for r in range(0, CB, 16):
            wanted = small(lax.broadcasted_iota(jnp.int32, (16, GBLOCK), 0) + r)
            lower_hit = wanted == along
            upper_hit = wanted == above
            for n, (low, up) in enumerate(shares):
                spread[n * CB + r : n * CB + r + 16, :] = jnp.where(
                    lower_hit, low, jnp.where(upper_hit, up, BF16(0.0))
                )

    def product(t, spread):
        rows = one_hot_rows(row_index(cell_ref[:, tile_of(t)]), GBLOCK)
        return lax.dot_general(
            rows, spread[...], (((1,), (1,)), ((), ())), preferred_element_type=F32
        )

    total = None
    slots = (va, vb)
    build(0, va)
    for t in range(blocks):
        if t + 1 < blocks:
            build(t + 1, slots[(t + 1) % 2])
        part = product(t, slots[t % 2])
        total = part if total is None else total + part
    total_ref[...] = total

    def settle(layer, carry):
        here = pl.ds(pl.multiple_of(layer * ACROSS, ACROSS), ACROSS)
        for odd in range(2):
            out_ref[field, layer, odd] = (
                total_ref[here, odd * HALF : (odd + 1) * HALF]
                + total_ref[here, CB + odd * HALF : CB + (odd + 1) * HALF]
            )
        return carry

    lax.fori_loop(0, CH, settle, 0)


def relax_kernel(
    slabs,
    count_ref,
    cell_ref,
    weight_ref,
    volume_ref,
    velocity_ref,
    p_ref,
    solid_ref,
    d_ref,
    total_ref,
    va,
    vb,
    terms_ref,
    gathered,
    coef,
    a_ref,
    b_ref,
    x0,
    x1,
    y0,
    z0,
    rs_send,
    rs_recv,
    ag_send,
    ag_recv,
    halo_send,
    halo_recv,
    p_send,
    p_recv,
):
    quad = lax.axis_index("quad")
    slab = lax.axis_index("slab")
    nexts = lax.rem(slab + 1, slabs)
    prevs = lax.rem(slab + slabs - 1, slabs)
    peers = [lax.rem(quad + d, QUADS) for d in range(QUADS)]
    origins = [lax.rem(quad + QUADS - d, QUADS) for d in range(QUADS)]

    def at(q, s):
        return {"quad": q, "slab": s}

    def rows_of(q):
        return pl.ds(pl.multiple_of(q * CA, CA), CA)

    barrier = pltpu.get_barrier_semaphore()
    has_prev = slab > 0
    has_next = slab < slabs - 1

    def greet(where):
        pl.semaphore_signal(
            barrier, inc=1, device_id=where, device_id_type=pl.DeviceIdType.MESH
        )

    for d in range(1, QUADS):
        greet(at(peers[d], slab))

    @pl.when(has_next)
    def _():
        greet(at(quad, nexts))

    @pl.when(has_prev)
    def _():
        greet(at(quad, prevs))

    def link(src, dst, ssem, rsem, where):
        return pltpu.make_async_remote_copy(
            src_ref=src,
            dst_ref=dst,
            send_sem=ssem,
            recv_sem=rsem,
            device_id=where,
            device_id_type=pl.DeviceIdType.MESH,
        )

    def send(*args):
        copy = link(*args)
        copy.start()
        return copy

    def each_side(copies, up, down):
        @pl.when(has_next)
        def _():
            up(copies[0])

        @pl.when(has_prev)
        def _():
            down(copies[1])

    def start(copies):
        each_side(copies, lambda c: c.start(), lambda c: c.start())

    def sent(copies):
        each_side(copies, lambda c: c.wait_send(), lambda c: c.wait_send())

    def arrived(copies):
        each_side(copies[::-1], lambda c: c.wait_recv(), lambda c: c.wait_recv())

    scatter, gather, halos = [], [], []
    for f in range(2):
        deposit(f, count_ref, cell_ref, weight_ref, volume_ref, velocity_ref, d_ref, total_ref, va, vb)
        if f == 0:
            callers = QUADS - 1 + has_prev.astype(jnp.int32) + has_next.astype(jnp.int32)
            pl.semaphore_wait(barrier, callers)
        scatter.append(
            {
                d: send(
                    d_ref.at[f, :, :, rows_of(peers[d]), :],
                    gathered.at[f, d - 1],
                    rs_send.at[f, d - 1],
                    rs_recv.at[f, d - 1],
                    at(peers[d], slab),
                )
                for d in (2, 1, 3)
            }
        )
    for buffer in (x0, x1, y0, z0, p_ref):
        rim = jnp.zeros((buffer.shape[0], 2, PAD, 128), F32)
        buffer[:, :, :PAD, :] = rim
        buffer[:, :, PAD + ACROSS :, :] = rim

    @pl.when(slab == 0)
    def _():
        for field in range(2):
            coef[field, 0:4] = jnp.zeros((4, 2, ACROSS, 128), F32)
        for buffer in (y0, z0):
            buffer[0:4] = jnp.zeros((4, 2, HELD, 128), F32)

    @pl.when(slab == slabs - 1)
    def _():
        for field in range(2):
            coef[field, 8:12] = jnp.zeros((4, 2, ACROSS, 128), F32)
        for buffer in (y0, z0):
            buffer[8:12] = jnp.zeros((4, 2, HELD, 128), F32)

    own = rows_of(quad)

    def forward(f, d):
        block = rows_of(origins[d])
        src = coef.at[f, 4:8, :, block, :]
        pair = [
            link(
                src,
                coef.at[f, low : low + 4, :, block, :],
                halo_send.at[f, side, d],
                halo_recv.at[f, side, d],
                at(quad, where),
            )
            for side, (low, where) in enumerate(((0, nexts), (8, prevs)))
        ]
        start(pair)
        halos.append(pair)

    for f in range(2):
        for copy in scatter[f].values():
            copy.wait_recv()
        coef[f, 4:8, :, own, :] = (d_ref[f, :, :, own, :] + gathered[f, 0]) + (
            gathered[f, 1] + gathered[f, 2]
        )
        mine = coef.at[f, 4:8, :, own, :]
        gather.append(
            {
                d: send(mine, mine, ag_send.at[f, d - 1], ag_recv.at[f, d - 1], at(peers[d], slab))
                for d in (2, 1, 3)
            }
        )
        forward(f, 0)
    for f in range(2):
        for d in (1, 3, 2):
            gather[f][d].wait_recv()
            forward(f, d)

    lane = lax.broadcasted_iota(jnp.int32, (ACROSS, 128), 1)
    inner = slice(PAD, PAD + ACROSS)

    def coefficients(k, carry):
        inside = jnp.logical_and(
            jnp.logical_or(k >= 4, has_prev), jnp.logical_or(k <= 7, has_next)
        )
        thick = 1.0 + coef[0, k]
        ratio = jnp.where(inside, 1.0, 0.0) / (6.0 + 0.05 * thick)
        source = 4.0 * coef[1, k] * thick * ratio
        b_ref[k] = ratio
        a_ref[k] = source
        x0[k, :, inner, :] = source
        return carry

    lax.fori_loop(4, 8, coefficients, 0)
    for pair in halos:
        arrived(pair)
    lax.fori_loop(0, 4, coefficients, 0)
    lax.fori_loop(8, 12, coefficients, 0)
    def sweep(src, dst, begin, end, shift=0):
        half = (end - begin) // 2

        def body(i, carry):
            for j in range(half):
                k = begin + half * i + j
                for odd in range(2):
                    other = src[k, 1 - odd, inner, :]
                    if odd:
                        turned = jnp.where(lane < 127, pltpu.roll(other, 127, axis=1), 0.0)
                    else:
                        turned = jnp.where(lane > 0, pltpu.roll(other, 1, axis=1), 0.0)
                    total = src[k - 1, odd, inner, :] + src[k + 1, odd, inner, :]
                    total += src[k, odd, PAD - 1 : PAD + ACROSS - 1, :]
                    total += src[k, odd, PAD + 1 : PAD + ACROSS + 1, :]
                    total += other + turned
                    dst[k - shift, odd, inner, :] = a_ref[k, odd] + b_ref[k, odd] * total
            return carry

        lax.fori_loop(0, 2, body, 0)

    def exchange(buffer, n):
        def block(low):
            return buffer.at[low : low + 4, :, PAD : PAD + ACROSS, :]

        src = block(4)
        pair = [
            link(src, block(0), p_send.at[n, 0], p_recv.at[n, 0], at(quad, nexts)),
            link(src, block(8), p_send.at[n, 1], p_recv.at[n, 1], at(quad, prevs)),
        ]
        start(pair)
        return pair

    sweep(x0, x1, 1, 11)
    sweep(x1, x0, 2, 10)
    sweep(x0, x1, 3, 9)
    sweep(x1, y0, 4, 8)
    early = exchange(y0, 0)
    for pair in range(2):
        for odd in range(2):
            block = [coef[0, 4 + 2 * pair + j, odd] for j in range(2)]
            store_split(block, terms_ref, 0, 1, pair, odd)

    def keep(tile, sampled):
        solid_ref[:, tile] = sampled[0]

    sample(cell_ref, weight_ref, terms_ref, 1, keep)
    arrived(early)
    sweep(y0, x0, 1, 11)
    sweep(x0, x1, 2, 10)
    sweep(x1, x0, 3, 9)
    sweep(x0, z0, 4, 8)
    later = exchange(z0, 1)
    arrived(later)
    sweep(z0, x0, 1, 11)
    sweep(x0, x1, 2, 10)
    sweep(x1, p_ref, 3, 9, shift=3)

    for copies in scatter + gather:
        for copy in copies.values():
            copy.wait_send()
    for pair in halos + [early, later]:
        sent(pair)


def store_split(blocks, terms_ref, f, fields, pair, odd):
    hi, lo = split(jnp.concatenate(blocks, axis=0).T)
    r = f * CB + odd * HALF
    lanes = slice(pair * 128, (pair + 1) * 128)
    terms_ref[r : r + HALF, lanes] = hi
    terms_ref[r + fields * CB : r + fields * CB + HALF, lanes] = lo


def sample(cell_ref, weight_ref, terms_ref, fields, done):
    def one(base):
        tile = pl.ds(base, GTILE)
        rows = one_hot_rows(row_index(cell_ref[:, tile]), GTILE)
        weight = weight_ref[:, tile]
        upper = 1.0 - weight
        along, above = keys(cell_ref[:, tile])
        wanted = lax.broadcasted_iota(jnp.int32, (CB, GTILE), 0)
        pick = jnp.where(wanted == along, weight, jnp.where(wanted == above, upper, 0.0))
        both = jnp.dot(terms_ref[...], rows, preferred_element_type=F32)
        picked = both[: fields * CB] + both[fields * CB :]
        done(
            tile,
            [
                jnp.sum(pick * picked[f * CB : (f + 1) * CB], axis=0, keepdims=True)
                for f in range(fields)
            ],
        )

    def body(i, carry):
        for j in range(UNROLL):
            one(pl.multiple_of((i * UNROLL + j) * GTILE, GTILE))
        return carry

    lax.fori_loop(0, cell_ref.shape[1] // (GTILE * UNROLL), body, 0)


def sample_kernel(
    count_ref,
    cell_ref,
    weight_ref,
    volume_ref,
    velocity_ref,
    p_ref,
    solid_ref,
    pressure_ref,
    drag_ref,
    terms_ref,
    turned,
):
    lane = lax.broadcasted_iota(jnp.int32, (ACROSS, 128), 1)
    inner = slice(PAD, PAD + ACROSS)
    for pair in range(2):
        for odd in range(2):
            blocks = [[], [], []]
            for k in (2 * pair + 1, 2 * pair + 2):
                other = p_ref[k, 1 - odd, inner, :]
                if odd:
                    right, left = jnp.where(lane < 127, pltpu.roll(other, 127, axis=1), 0.0), other
                else:
                    right, left = other, jnp.where(lane > 0, pltpu.roll(other, 1, axis=1), 0.0)
                blocks[0].append(-0.5 * (p_ref[k + 1, odd, inner, :] - p_ref[k - 1, odd, inner, :]))
                blocks[1].append(
                    -0.5
                    * (
                        p_ref[k, odd, PAD + 1 : PAD + ACROSS + 1, :]
                        - p_ref[k, odd, PAD - 1 : PAD + ACROSS - 1, :]
                    )
                )
                blocks[2].append(-0.5 * (right - left))
            for f in range(3):
                store_split(blocks[f], terms_ref, f, 3, pair, odd)
    quad = lax.axis_index("quad")
    mine = pl.ds(pl.multiple_of(PAD + quad * CA, PAD), CA)
    swapped = jnp.concatenate(
        [p_ref[k + 1, odd, mine, :] for odd in range(2) for k in range(CH)], axis=0
    ).T
    turned[pl.ds(0, HALF, stride=2), :] = swapped
    turned[pl.ds(1, HALF, stride=2), :] = pltpu.roll(swapped, 64, axis=1)
    whole = turned[...].T
    for k in range(CH):
        pressure_ref[k] = whole[k * CA : (k + 1) * CA]

    def finish(tile, sampled):
        slots = tile.start + lax.broadcasted_iota(jnp.int32, (1, GTILE), 1)
        mass = jnp.where(slots < count_ref[...], volume_ref[:, tile], 0.0)
        factor = mass * (1.0 + solid_ref[:, tile]) ** 2
        for f in range(3):
            drag_ref[f : f + 1, tile] = factor * (sampled[f] - velocity_ref[f : f + 1, tile])

    sample(cell_ref, weight_ref, terms_ref, 3, finish)


def body(slabs, grain_cell, grain_count, grain_weight, grain_volume, grain_velocity):
    grains = grain_weight.shape[0]
    weight = grain_weight.reshape(1, grains)
    volume = grain_volume.reshape(1, grains)
    count = grain_count.reshape(1, 1)
    vmem = pl.BlockSpec(memory_space=pltpu.VMEM)
    dma = pltpu.SemaphoreType.DMA
    pressure, solid = pl.pallas_call(
        functools.partial(relax_kernel, slabs),
        out_shape=(
            jax.ShapeDtypeStruct((CH + 2, 2, HELD, 128), F32),
            jax.ShapeDtypeStruct((1, grains), F32),
        ),
        in_specs=[vmem] * 5,
        out_specs=(vmem, vmem),
        scratch_shapes=[
            pltpu.VMEM((2, CH, 2, ACROSS, 128), F32),
            pltpu.VMEM((ROWS, 2 * CB), F32),
            pltpu.VMEM((2 * CB, GBLOCK), BF16),
            pltpu.VMEM((2 * CB, GBLOCK), BF16),
            pltpu.VMEM((2 * CB, ROWS), BF16),
            pltpu.VMEM((2, 3, CH, 2, CA, 128), F32),
            pltpu.VMEM((2, 3 * CH, 2, ACROSS, 128), F32),
            pltpu.VMEM((3 * CH, 2, ACROSS, 128), F32),
            pltpu.VMEM((3 * CH, 2, ACROSS, 128), F32),
        ]
        + [pltpu.VMEM((3 * CH, 2, HELD, 128), F32)] * 4
        + [dma((2, 3))] * 4
        + [dma((2, 2, QUADS))] * 2
        + [dma((2, 2))] * 2,
        compiler_params=pltpu.CompilerParams(collective_id=0, has_side_effects=True),
        name="relax",
    )(count, grain_cell, weight, volume, grain_velocity)
    return pl.pallas_call(
        sample_kernel,
        out_shape=(
            jax.ShapeDtypeStruct((CH, CA, CB), F32),
            jax.ShapeDtypeStruct((3, grains), F32),
        ),
        in_specs=[vmem] * 7,
        out_specs=(vmem, vmem),
        scratch_shapes=[
            pltpu.VMEM((6 * CB, ROWS), BF16),
            pltpu.VMEM((CB, 128), F32),
        ],
        name="sample",
    )(count, grain_cell, weight, volume, grain_velocity, pressure, solid)


def solution(mesh):
    placed = (
        P(None, ("slab", "quad")),
        P(("slab", "quad")),
        P(("slab", "quad")),
        P(("slab", "quad")),
        P(None, ("slab", "quad")),
    )
    return jax.shard_map(
        functools.partial(body, mesh.shape["slab"]),
        mesh=mesh,
        in_specs=placed,
        out_specs=(P("slab", "quad", None), P(None, ("slab", "quad"))),
        check_vma=False,
    )
```
